32 devices in a mesh: grp: 2 (over core), tp: 8 (over z, y), dp: 2 (over x).
Axes of the slice: x: 2, y: 2, z: 4, core: 2. Of those that a mesh axis runs over, the one named last changes fastest.
Arguments:
- base_inputs: bfloat16 [3, 128, 8192], P(None, 'dp', ('grp', 'tp')), may hold values from -6 to 6
- small_inputs: bfloat16 [2, 3, 128, 4096], P('grp', None, 'dp', 'tp'), may hold values from -6 to 6
- base_norm_gain: float32 [8192], replicated, may hold values from 0.1 to 1.9
- base_query: bfloat16 [8192, 8192], P(None, ('grp', 'tp')), may hold values from -0.0625 to 0.0625
- base_keys_values: bfloat16 [2, 8192, 1024], P(None, None, ('grp', 'tp')), may hold values from -0.0625 to 0.0625
- base_output: bfloat16 [8192, 8192], P(('grp', 'tp')), may hold values from -0.0625 to 0.0625
- base_cache: bfloat16 [2, 128, 1024, 128], P(None, 'dp', ('grp', 'tp')), may hold values from -600 to 600
- base_final_gain: float32 [8192], replicated, may hold values from 0.1 to 1.9
- base_unembed: bfloat16 [16384, 8192], P(('grp', 'tp')), may hold values from -20 to 20
- small_norm_gain: float32 [2, 4096], P('grp'), may hold values from 0.1 to 1.9
- small_projections: bfloat16 [2, 3, 4096, 4096], P('grp', None, None, 'tp'), may hold values from -0.09375 to 0.09375
- small_output: bfloat16 [2, 4096, 4096], P('grp', 'tp'), may hold values from -0.09375 to 0.09375
- small_cache: bfloat16 [2, 2, 128, 4096, 128], P('grp', None, 'dp', 'tp'), may hold values from -600 to 600
- small_final_gain: float32 [2, 4096], P('grp'), may hold values from 0.1 to 1.9
- small_unembed: bfloat16 [2, 2, 8192, 4096], P('grp', None, 'tp'), may hold values from -0.1875 to 0.1875
- lengths: int32 [128], P('dp'), may hold values from 1 to 128, as said below
- next_tokens: int32 [3, 128], P(None, 'dp'), may hold values from 0 to 16383
Outputs:
- log_probs: float32 [3, 128, 16384], P(None, 'dp', ('grp', 'tp'))
- chosen_total: float32 [128], P('dp')
The draws below stay inside these ranges and needn't reach their ends.
Inputs may be any that keep to these rules, and one draw needn't show every extreme that they name: `lengths`: some row holds 128 cached positions.
All inputs are finite; a program needn't handle non-finite values.
Results may differ from the reference program's by a relative error of at most 0.0035.
Values may be sent and summed in bfloat16 or wider, within the bound.
A program may use at most 256 MiB of HBM per device.

```python
import math
import jax
import jax.numpy as jnp
from jax import lax

DB = 8192
HB = 64
KVB = 8
HD = 128
DS = 4096
HS = 32
VOCAB = 16384
STEPS = 3
CACHE = 128
ROWS = 128
N_GRP = 2
N_TP = 8


def cache_draw(key, full_shape):
    key_entries = jax.random.fold_in(key, 0)
    entries = jnp.clip(jax.random.normal(key_entries, full_shape, jnp.float32), -6.0, 6.0)
    key_factor = jnp.ones((ROWS, 1, CACHE), jnp.float32)
    factor = jnp.stack([key_factor, jnp.full((ROWS, 1, CACHE), 3.0, jnp.float32)], axis=0)
    return (entries * factor).astype(jnp.bfloat16)


def draw_base_cache(key, part):
    return cache_draw(key, (2, ROWS, KVB * HD, CACHE))


def draw_small_cache(key, part):
    return cache_draw(key, (2, 2, ROWS, HS * HD, CACHE))


def draw_base_unembed(key, part):
    key_entries = jax.random.fold_in(key, 0)
    spread = 3.0 / math.sqrt(DB)
    entries = jnp.clip(jax.random.normal(key_entries, (VOCAB, DB), jnp.float32), -6.0, 6.0) * spread
    return entries.astype(jnp.bfloat16)


def draw_lengths(key, part):
    key_values, key_spot = jax.random.split(key, 2)
    drawn = jax.random.randint(key_values, (ROWS,), 1, CACHE + 1)
    longest = jax.random.randint(key_spot, (), 0, ROWS)
    return jnp.where(jnp.arange(ROWS) == longest, CACHE, drawn).astype(jnp.int32)


def place_ends(result, rng, least, largest):
    extent = result.shape
    place = [jax.random.randint(jax.random.fold_in(rng, axis), (), 0, extent[axis]) for axis in range(len(extent))]
    result = result.at[tuple(place)].set(least)
    longest = extent.index(max(extent))
    place[longest] = (place[longest] + 1) % extent[longest]
    return result.at[tuple(place)].set(largest)


def block_levels(key, extent, pieces, least, high):
    gain = 1.0
    for dim, parts in pieces:
        draws = jax.random.uniform(jax.random.fold_in(jax.random.fold_in(key, 6), dim), (parts,), jnp.float32, least / len(pieces), high / len(pieces))
        gain = gain * jnp.repeat(jnp.exp(draws), extent[dim] // parts).reshape((-1,) + (1,) * (len(extent) - 1 - dim))
    return gain


def centred(stream_key, dims, scale, most, cuts=(), kind=jnp.bfloat16):
    values = scale * jax.random.normal(stream_key, dims, jnp.float32)
    if cuts:
        values = values * block_levels(stream_key, dims, cuts, -0.22, 0.18)
    return jnp.clip(values, -most, most).astype(kind)


def setup_inputs(seed: int = 0) -> dict:
    arg_keys = jax.random.split(jax.random.key(seed), 18)
    base_inputs = centred(arg_keys[0], (STEPS, ROWS, DB), 1.0, 6.0, ((1, 2), (2, 16)))
    small_inputs = centred(arg_keys[1], (2, STEPS, ROWS, DS), 1.0, 6.0, ((0, 2), (2, 2), (3, 8)))
    base_norm_gain = jnp.clip(1.0 + 0.18 * jax.random.normal(arg_keys[2], (DB,), jnp.float32), 0.1, 1.9)
    base_query = centred(arg_keys[3], (DB, HB * HD), DB ** -0.5, 0.0625, ((1, 16),))
    base_keys_values = centred(arg_keys[4], (2, DB, KVB * HD), DB ** -0.5, 0.0625, ((2, 16),))
    base_output = centred(arg_keys[5], (HB * HD, DB), (HB * HD) ** -0.5, 0.0625, ((0, 16),))
    base_cache = draw_base_cache(jax.random.fold_in(arg_keys[17], 71), 0)
    base_final_gain = jnp.clip(1.0 + 0.18 * jax.random.normal(arg_keys[7], (DB,), jnp.float32), 0.1, 1.9)
    base_unembed = draw_base_unembed(jax.random.fold_in(arg_keys[17], 71), 0)
    small_norm_gain = jnp.clip(1.0 + 0.18 * jax.random.normal(arg_keys[9], (2, DS), jnp.float32), 0.1, 1.9)
    small_projections = centred(arg_keys[10], (2, 3, DS, HS * HD), DS ** -0.5, 0.09375, ((0, 2), (3, 8)))
    small_output = centred(arg_keys[11], (2, HS * HD, DS), (HS * HD) ** -0.5, 0.09375, ((0, 2), (1, 8)))
    small_cache = draw_small_cache(jax.random.fold_in(arg_keys[17], 71), 0)
    small_final_gain = jnp.clip(1.0 + 0.18 * jax.random.normal(arg_keys[13], (2, DS), jnp.float32), 0.1, 1.9)
    small_unembed = centred(arg_keys[14], (2, 2, VOCAB // 2, DS), (DS // 4) ** -0.5, 0.1875, ((0, 2), (2, 8)))
    lengths = draw_lengths(jax.random.fold_in(arg_keys[17], 71), 0)
    next_tokens = place_ends(jax.random.randint(arg_keys[16], (STEPS, ROWS), 0, VOCAB), jax.random.fold_in(arg_keys[16], 1), 0, VOCAB - 1).astype(jnp.int32)
    return dict(base_inputs=base_inputs, small_inputs=small_inputs, base_norm_gain=base_norm_gain, base_query=base_query, base_keys_values=base_keys_values, base_output=base_output, base_cache=base_cache, base_final_gain=base_final_gain, base_unembed=base_unembed, small_norm_gain=small_norm_gain, small_projections=small_projections, small_output=small_output, small_cache=small_cache, small_final_gain=small_final_gain, small_unembed=small_unembed, lengths=lengths, next_tokens=next_tokens)


EPSILON = 1e-05
NEGATIVE = -1e+30

def rotate_pairs(values, positions, first_pair, head_size):
    pair_count = values.shape[-1] // 2
    pair_index = (first_pair + jnp.arange(pair_count)).astype(jnp.float32)
    frequency = jnp.exp(pair_index * (-2.0 * math.log(10000.0) / head_size))
    angles = positions.astype(jnp.float32)[:, None] * frequency[None, :]
    angles = angles.reshape((values.shape[0],) + (1,) * (values.ndim - 2) + (pair_count,))
    cosine = jnp.cos(angles)
    sine_part = jnp.sin(angles)
    paired = values.reshape(values.shape[:-1] + (pair_count, 2))
    even_part = paired[..., 0]
    odd_part = paired[..., 1]
    turned = jnp.stack([even_part * cosine - odd_part * sine_part, even_part * sine_part + odd_part * cosine], axis=-1)
    return turned.reshape(values.shape)

def norm_rows(values, gain_row):
    values = values.astype(jnp.float32)
    scaling = lax.rsqrt(lax.optimization_barrier(jnp.mean(values * values, axis=-1, keepdims=True)) + EPSILON)
    return (values * scaling * gain_row).astype(jnp.bfloat16)

def attention_weights(cached_scores, fresh_scores, visible, head_size):
    factor = 1.0 / math.sqrt(head_size)
    cached_scores = jnp.where(visible, cached_scores * factor, NEGATIVE)
    fresh_scores = fresh_scores * factor
    row_max = jnp.maximum(lax.optimization_barrier(jnp.max(cached_scores, axis=-1, keepdims=True)), lax.optimization_barrier(jnp.max(fresh_scores, axis=-1, keepdims=True)))
    cached_exp = jnp.exp(cached_scores - row_max)
    fresh_exp = jnp.exp(fresh_scores - row_max)
    totals = lax.optimization_barrier(jnp.sum(cached_exp, axis=-1, keepdims=True)) + lax.optimization_barrier(jnp.sum(fresh_exp, axis=-1, keepdims=True))
    return ((cached_exp / totals).astype(jnp.bfloat16), (fresh_exp / totals).astype(jnp.bfloat16))

def small_model(model_index, small_inputs, lengths, small_norm_gain, small_projections, small_output, small_cache, small_final_gain, small_unembed):
    visible = (jnp.arange(CACHE)[None, :] < lengths[:, None])[:, None, :]
    keys_cached = small_cache[model_index, 0].reshape(ROWS, HS, HD, CACHE).astype(jnp.float32)
    values_cached = small_cache[model_index, 1].reshape(ROWS, HS, HD, CACHE).astype(jnp.float32)
    vocab_table = small_unembed[model_index].reshape(VOCAB, DS)
    new_keys = []
    new_values = []
    logit_steps = []
    for step_index in range(STEPS):
        positions = lengths + step_index
        inputs_now = small_inputs[model_index, step_index]
        normed = norm_rows(inputs_now, small_norm_gain[model_index])
        queries = jnp.dot(normed, small_projections[model_index, 0], preferred_element_type=jnp.float32).reshape(ROWS, HS, HD)
        queries = rotate_pairs(queries, positions, 0, HD).astype(jnp.bfloat16)
        new_key = jnp.dot(normed, small_projections[model_index, 1], preferred_element_type=jnp.float32).reshape(ROWS, HS, HD)
        new_keys.append(rotate_pairs(new_key, positions, 0, HD).astype(jnp.bfloat16))
        new_value = jnp.dot(normed, small_projections[model_index, 2], preferred_element_type=jnp.float32).reshape(ROWS, HS, HD)
        new_values.append(new_value.astype(jnp.bfloat16))
        fresh_keys = jnp.stack(new_keys, axis=-1).astype(jnp.float32)
        fresh_values = jnp.stack(new_values, axis=-1).astype(jnp.float32)
        queries_wide = queries.astype(jnp.float32)
        cached_scores = jnp.einsum('rhd,rhdl->rhl', queries_wide, keys_cached)
        fresh_scores = jnp.einsum('rhd,rhdn->rhn', queries_wide, fresh_keys)
        cached_weights, fresh_weights = attention_weights(cached_scores, fresh_scores, visible, HD)
        head_values = jnp.einsum('rhl,rhdl->rhd', cached_weights.astype(jnp.float32), values_cached)
        head_values = head_values + jnp.einsum('rhn,rhdn->rhd', fresh_weights.astype(jnp.float32), fresh_values)
        head_values = head_values.astype(jnp.bfloat16).reshape(ROWS, HS * HD)
        hidden = inputs_now.astype(jnp.float32) + jnp.dot(head_values, small_output[model_index], preferred_element_type=jnp.float32)
        final_rows = norm_rows(hidden, small_final_gain[model_index])
        logit_steps.append(jnp.dot(final_rows, vocab_table.T, preferred_element_type=jnp.float32))
    return logit_steps

def base_model(base_inputs, lengths, base_norm_gain, base_query, base_keys_values, base_output, base_cache, base_final_gain, base_unembed):
    share_count = N_GRP * N_TP // KVB
    slice_width = HD // share_count
    group_size = HB // KVB
    visible = (jnp.arange(CACHE)[None, :] < lengths[:, None])[:, None, None, :]
    keys_cached = base_cache[0].reshape(ROWS, KVB, HD, CACHE).astype(jnp.float32)
    values_cached = base_cache[1].reshape(ROWS, KVB, HD, CACHE).astype(jnp.float32)
    new_keys = []
    new_values = []
    logit_steps = []
    for step_index in range(STEPS):
        positions = lengths + step_index
        inputs_now = base_inputs[step_index]
        normed = norm_rows(inputs_now, base_norm_gain)
        queries = jnp.dot(normed, base_query, preferred_element_type=jnp.float32)
        queries = queries.reshape(ROWS, KVB, share_count, group_size, slice_width).transpose(0, 1, 3, 2, 4).reshape(ROWS, KVB, group_size, HD)
        queries = rotate_pairs(queries, positions, 0, HD).astype(jnp.bfloat16)
        new_key = jnp.dot(normed, base_keys_values[0], preferred_element_type=jnp.float32).reshape(ROWS, KVB, HD)
        new_keys.append(rotate_pairs(new_key, positions, 0, HD).astype(jnp.bfloat16))
        new_value = jnp.dot(normed, base_keys_values[1], preferred_element_type=jnp.float32).reshape(ROWS, KVB, HD)
        new_values.append(new_value.astype(jnp.bfloat16))
        fresh_keys = jnp.stack(new_keys, axis=-1).astype(jnp.float32)
        fresh_values = jnp.stack(new_values, axis=-1).astype(jnp.float32)
        queries_wide = queries.astype(jnp.float32)
        cached_scores = jnp.einsum('rkgd,rkdl->rkgl', queries_wide, keys_cached)
        fresh_scores = jnp.einsum('rkgd,rkdn->rkgn', queries_wide, fresh_keys)
        cached_weights, fresh_weights = attention_weights(cached_scores, fresh_scores, visible, HD)
        head_values = jnp.einsum('rkgl,rkdl->rkgd', cached_weights.astype(jnp.float32), values_cached)
        head_values = head_values + jnp.einsum('rkgn,rkdn->rkgd', fresh_weights.astype(jnp.float32), fresh_values)
        head_values = head_values.astype(jnp.bfloat16).reshape(ROWS, KVB, group_size, share_count, slice_width)
        head_values = head_values.transpose(0, 1, 3, 2, 4).reshape(ROWS, HB * HD)
        hidden = inputs_now.astype(jnp.float32) + jnp.dot(head_values, base_output, preferred_element_type=jnp.float32)
        final_rows = norm_rows(hidden, base_final_gain)
        logit_steps.append(jnp.dot(final_rows, base_unembed.T, preferred_element_type=jnp.float32))
    return logit_steps

def reference(base_inputs, small_inputs, base_norm_gain, base_query, base_keys_values, base_output, base_cache, base_final_gain, base_unembed, small_norm_gain, small_projections, small_output, small_cache, small_final_gain, small_unembed, lengths, next_tokens):
    expert_steps = small_model(0, small_inputs, lengths, small_norm_gain, small_projections, small_output, small_cache, small_final_gain, small_unembed)
    anti_steps = small_model(1, small_inputs, lengths, small_norm_gain, small_projections, small_output, small_cache, small_final_gain, small_unembed)
    base_steps = base_model(base_inputs, lengths, base_norm_gain, base_query, base_keys_values, base_output, base_cache, base_final_gain, base_unembed)
    log_steps = []
    chosen_total = jnp.zeros((ROWS,), jnp.float32)
    for step_index in range(STEPS):
        steered = base_steps[step_index] + expert_steps[step_index] - anti_steps[step_index]
        row_max = lax.optimization_barrier(jnp.max(steered, axis=-1, keepdims=True))
        log_norm = row_max + jnp.log(lax.optimization_barrier(jnp.sum(jnp.exp(steered - row_max), axis=-1, keepdims=True)))
        step_probs = steered - log_norm
        log_steps.append(step_probs)
        chosen_total = chosen_total + jnp.take_along_axis(step_probs, next_tokens[step_index][:, None].astype(jnp.int32), axis=1)[:, 0]
    return (jnp.stack(log_steps, axis=0), chosen_total)
```

```python
import functools
import math

import jax
import jax.numpy as jnp
from jax import lax
from jax.experimental import pallas as pl
from jax.experimental.pallas import tpu as pltpu
from jax.sharding import PartitionSpec as P

HD = 128
STEPS = 3
CACHE = 128


EPSILON = 1e-05
NEGATIVE = -1e30
VMEM_LIMIT = 48 * 1024 * 1024


def partner(array, axis, bit):
    return lax.ppermute(array, axis, [(i, i ^ 1 << bit) for i in range(lax.axis_size(axis))])


def tile_of(size, most):
    tile = min(size, most)
    while size % tile:
        tile //= 2
    return tile


def rotation_tables(positions, first_pair, width, head_size):
    pair_index = (first_pair + jnp.arange(width) // 2).astype(jnp.float32)
    frequency = jnp.exp(pair_index * (-2.0 * math.log(10000.0) / head_size))
    angles = positions.astype(jnp.float32)[:, None] * frequency[None, :]
    sign = jnp.where(jnp.arange(width) % 2 == 0, -1.0, 1.0)
    return jnp.cos(angles), jnp.sin(angles) * sign


def rotate(values, cosine, sine):
    copies = values.shape[1] // cosine.shape[1]
    cosine = jnp.tile(cosine, (1, copies))
    sine = jnp.tile(sine, (1, copies))
    even = (jnp.arange(values.shape[1]) % 2 == 0)[None, :]
    other = jnp.where(even, jnp.roll(values, -1, axis=1), jnp.roll(values, 1, axis=1))
    return (values * cosine + other * sine).astype(jnp.bfloat16)


def norm_rows(values, gain_row):
    values = values.astype(jnp.float32)
    scaling = lax.rsqrt(jnp.mean(values * values, axis=-1, keepdims=True) + EPSILON)
    return (values * scaling * gain_row).astype(jnp.bfloat16)


def project_kernel(tile, weight_count, x_ref, gain_ref, *refs):
    weights = refs[:weight_count]
    outs = refs[weight_count:-1]
    scale_ref = refs[-1]
    step = pl.program_id(0)
    rows, depth = x_ref.shape

    @pl.when(step == 0)
    def _():
        def add(index, total):
            part = x_ref[:, pl.ds(pl.multiple_of(index * tile, tile), tile)].astype(jnp.float32)
            return total + jnp.sum(part * part, axis=-1, keepdims=True)

        total = lax.fori_loop(0, depth // tile, add, jnp.zeros((rows, 1), jnp.float32))
        scaling = lax.rsqrt(total / depth + EPSILON)
        scale_ref[...] = jnp.broadcast_to(scaling, scale_ref.shape)
        for out in outs:
            out[...] = jnp.zeros_like(out)

    columns = pl.ds(pl.multiple_of(step * tile, tile), tile)
    normed = x_ref[:, columns].astype(jnp.float32) * scale_ref[:, :1] * gain_ref[:, columns]
    normed = normed.astype(jnp.bfloat16)
    place = 0
    for weight in weights:
        if len(weight.shape) == 2:
            outs[place][...] += jnp.dot(normed, weight[...], preferred_element_type=jnp.float32)
            place += 1
        else:
            for index in range(weight.shape[0]):
                outs[place][...] += jnp.dot(
                    normed, weight[index], preferred_element_type=jnp.float32
                )
                place += 1


def project(x, gain, weights, tile):
    rows, depth = x.shape
    tile = tile_of(depth, tile)
    specs = []
    shapes = []
    for weight in weights:
        width = weight.shape[-1]
        if weight.ndim == 2:
            specs.append(pl.BlockSpec((tile, width), lambda k: (k, 0)))
            shapes.append((rows, width))
        else:
            specs.append(pl.BlockSpec((weight.shape[0], tile, width), lambda k: (0, k, 0)))
            shapes.extend([(rows, width)] * weight.shape[0])
    return pl.pallas_call(
        functools.partial(project_kernel, tile, len(weights)),
        grid=(depth // tile,),
        in_specs=[
            pl.BlockSpec((rows, depth), lambda k: (0, 0)),
            pl.BlockSpec((1, depth), lambda k: (0, 0)),
        ]
        + specs,
        out_specs=[pl.BlockSpec(shape, lambda k: (0, 0)) for shape in shapes],
        out_shape=[jax.ShapeDtypeStruct(shape, jnp.float32) for shape in shapes],
        scratch_shapes=[pltpu.VMEM((rows, 128), jnp.float32)],
        compiler_params=pltpu.CompilerParams(vmem_limit_bytes=VMEM_LIMIT),
    )(x, gain, *weights)


def out_kernel(x_ref, w_ref, o_ref):
    o_ref[...] = jnp.dot(x_ref[...], w_ref[...], preferred_element_type=jnp.float32).astype(
        o_ref.dtype
    )


def out_project(x, weight, most):
    rows, depth = x.shape
    width = weight.shape[1]
    tile = tile_of(width, most)
    return pl.pallas_call(
        out_kernel,
        grid=(width // tile,),
        in_specs=[
            pl.BlockSpec((rows, depth), lambda n: (0, 0)),
            pl.BlockSpec((depth, tile), lambda n: (0, n)),
        ],
        out_specs=pl.BlockSpec((rows, tile), lambda n: (0, n)),
        out_shape=jax.ShapeDtypeStruct((rows, width), jnp.bfloat16),
        compiler_params=pltpu.CompilerParams(vmem_limit_bytes=VMEM_LIMIT),
    )(x, weight)


def logit_kernel(x_ref, w_ref, o_ref):
    o_ref[...] = lax.dot_general(
        x_ref[...], w_ref[...], (((1,), (1,)), ((), ())), preferred_element_type=jnp.float32
    )


def logit_project(x, table, most):
    rows, depth = x.shape
    parts, width = table.shape[:2]
    tile = tile_of(width, most)
    return pl.pallas_call(
        logit_kernel,
        grid=(parts, width // tile),
        in_specs=[
            pl.BlockSpec((rows, depth), lambda p, n: (0, 0)),
            pl.BlockSpec((None, tile, depth), lambda p, n: (p, n, 0)),
        ],
        out_specs=pl.BlockSpec((None, rows, tile), lambda p, n: (p, 0, n)),
        out_shape=jax.ShapeDtypeStruct((parts, rows, width), jnp.float32),
        compiler_params=pltpu.CompilerParams(vmem_limit_bytes=VMEM_LIMIT),
    )(x, table)


def attention_weights(cached_scores, fresh_scores, visible, causal):
    factor = 1.0 / math.sqrt(HD)
    cached_scores = jnp.where(visible, cached_scores * factor, NEGATIVE)
    fresh_scores = jnp.where(causal, fresh_scores * factor, NEGATIVE)
    row_max = jnp.maximum(
        jnp.max(cached_scores, axis=-1, keepdims=True),
        jnp.max(fresh_scores, axis=-1, keepdims=True),
    )
    cached_exp = jnp.exp(cached_scores - row_max)
    fresh_exp = jnp.exp(fresh_scores - row_max)
    totals = jnp.sum(cached_exp, axis=-1, keepdims=True) + jnp.sum(
        fresh_exp, axis=-1, keepdims=True
    )
    return ((cached_exp / totals).astype(jnp.bfloat16), (fresh_exp / totals).astype(jnp.bfloat16))


def mix_rows(partial, inputs, gain, axes):
    count = lax.axis_size(axes)
    rows = partial.shape[0] // count
    mixed = lax.psum_scatter(
        partial.reshape(count, rows, partial.shape[1]), axes, scatter_dimension=0, tiled=False
    )
    start = lax.axis_index(axes) * rows
    hidden = lax.dynamic_slice_in_dim(inputs, start, rows, 0).astype(jnp.float32) + mixed.astype(
        jnp.float32
    )
    final = norm_rows(hidden, gain)
    return lax.all_gather(final, axes, axis=0, tiled=False).reshape(partial.shape)


def body(
    base_inputs,
    small_inputs,
    base_norm_gain,
    base_query,
    base_keys_values,
    base_output,
    base_cache,
    base_final_gain,
    base_unembed,
    small_norm_gain,
    small_projections,
    small_output,
    small_cache,
    small_final_gain,
    small_unembed,
    lengths,
    next_tokens,
):
    row_count = lengths.shape[0]
    total_rows = STEPS * row_count
    slice_width = base_keys_values.shape[2]
    share_count = HD // slice_width
    group_size = base_query.shape[1] // slice_width
    slice_index = lax.axis_index("tp") % share_count
    first_pair = slice_index * (slice_width // 2)
    block_index = lax.axis_index(("grp", "tp"))
    vocab_width = base_unembed.shape[0]
    small_heads = small_projections.shape[3] // HD
    every = ("grp", "tp")
    small_full = lax.all_gather(small_inputs[0], "tp", axis=2, tiled=True)
    small_full = small_full.reshape(total_rows, -1)
    base_full = lax.all_gather(base_inputs, every, axis=2, tiled=True).reshape(total_rows, -1)
    positions = (jnp.arange(STEPS)[:, None] + lengths[None, :]).reshape(-1)
    visible = (jnp.arange(CACHE)[None, :] < lengths[:, None])[:, None, None, :]
    step_range = jnp.arange(STEPS)
    causal = step_range[None, :] <= step_range[:, None]

    small_q, small_k, small_v = project(
        small_full, small_norm_gain, [small_projections[0]], 512
    )
    cosine, sine = rotation_tables(positions, 0, HD, HD)
    by_head = (STEPS, row_count, small_heads, HD)
    small_q = rotate(small_q, cosine, sine).reshape(by_head)
    small_k = rotate(small_k, cosine, sine).reshape(by_head)
    small_v = small_v.astype(jnp.bfloat16).reshape(by_head)
    keys = small_cache[0, 0].reshape(row_count, small_heads, HD, CACHE)
    values = small_cache[0, 1].reshape(row_count, small_heads, HD, CACHE)
    cached = jnp.einsum("srhd,rhdl->rhsl", small_q, keys, preferred_element_type=jnp.float32)
    fresh = jnp.einsum("srhd,nrhd->rhsn", small_q, small_k, preferred_element_type=jnp.float32)
    cached, fresh = attention_weights(cached, fresh, visible, causal[None, None])
    heads = jnp.einsum("rhsl,rhdl->srhd", cached, values, preferred_element_type=jnp.float32)
    heads = heads + jnp.einsum(
        "rhsn,nrhd->srhd", fresh, small_v, preferred_element_type=jnp.float32
    )
    heads = heads.astype(jnp.bfloat16).reshape(total_rows, small_heads * HD)
    small_partial = out_project(heads, small_output[0], 1024)
    small_final = mix_rows(small_partial, small_full, small_final_gain[0], "tp")
    small_logits = logit_project(small_final, small_unembed[0], 512)
    group = lax.axis_index("grp")
    own = lax.dynamic_index_in_dim(small_logits, group, 0, keepdims=False)
    theirs = lax.dynamic_index_in_dim(small_logits, 1 - group, 0, keepdims=False)
    received = lax.ppermute(theirs, "grp", [(0, 1), (1, 0)])

    query, new_key, new_value = project(
        base_full, base_norm_gain[None], [base_query, base_keys_values], 1024
    )
    cosine, sine = rotation_tables(positions, first_pair, slice_width, HD)
    query = rotate(query, cosine, sine).reshape(STEPS, row_count, group_size, slice_width)
    new_key = rotate(new_key, cosine, sine).reshape(STEPS, row_count, slice_width)
    new_value = new_value.astype(jnp.bfloat16).reshape(STEPS, row_count, slice_width)
    cached = jnp.einsum("srgd,rdl->rsgl", query, base_cache[0], preferred_element_type=jnp.float32)
    fresh = jnp.einsum("srgd,nrd->rsgn", query, new_key, preferred_element_type=jnp.float32)
    for bit in range(share_count.bit_length() - 1):
        cached = cached + partner(cached, "tp", bit)
        fresh_flat = fresh.reshape(row_count, -1)
        fresh = fresh + partner(fresh_flat, "tp", bit).reshape(fresh.shape)
    cached, fresh = attention_weights(cached, fresh, visible, causal[:, None, :][None])
    heads = jnp.einsum("rsgl,rdl->srgd", cached, base_cache[1], preferred_element_type=jnp.float32)
    heads = heads + jnp.einsum(
        "rsgn,nrd->srgd", fresh, new_value, preferred_element_type=jnp.float32
    )
    heads = heads.astype(jnp.bfloat16).reshape(total_rows, group_size * slice_width)
    partial = out_project(heads, base_output, 1024)
    final_rows = mix_rows(partial, base_full, base_final_gain, every)
    base_logits = logit_project(final_rows, base_unembed[None], 256)[0]
    gap = jnp.where(group == 0, own - received, received - own)
    steered = base_logits + gap

    local_max = jnp.max(steered, axis=-1)
    local_total = jnp.sum(jnp.exp(steered - local_max[:, None]), axis=-1)
    token_local = next_tokens.reshape(-1) - block_index * vocab_width
    token_hit = jnp.arange(vocab_width)[None, :] == token_local[:, None]
    picked = jnp.sum(jnp.where(token_hit, steered, 0.0), axis=-1)
    stats = lax.all_gather(jnp.stack([local_max, local_total, picked]), every, axis=0)
    row_max = jnp.max(stats[:, 0], axis=0)
    exp_total = jnp.sum(stats[:, 1] * jnp.exp(stats[:, 0] - row_max[None]), axis=0)
    log_norm = row_max + jnp.log(exp_total)
    chosen = jnp.sum(stats[:, 2], axis=0) - log_norm
    log_probs = steered - log_norm[:, None]
    return (
        log_probs.reshape(STEPS, row_count, vocab_width),
        jnp.sum(chosen.reshape(STEPS, row_count), axis=0),
    )


def solution(mesh):
    placed = (
        P(None, "dp", ("grp", "tp")),
        P("grp", None, "dp", "tp"),
        P(),
        P(None, ("grp", "tp")),
        P(None, None, ("grp", "tp")),
        P(("grp", "tp"), None),
        P(None, "dp", ("grp", "tp"), None),
        P(),
        P(("grp", "tp"), None),
        P("grp", None),
        P("grp", None, None, "tp"),
        P("grp", "tp", None),
        P("grp", None, "dp", "tp", None),
        P("grp", None),
        P("grp", None, "tp", None),
        P("dp"),
        P(None, "dp"),
    )
    return jax.shard_map(
        body,
        mesh=mesh,
        in_specs=placed,
        out_specs=(P(None, "dp", ("grp", "tp")), P("dp")),
        check_vma=False,
    )
```

```python
import functools
import math

import jax
import jax.numpy as jnp
from jax import lax
from jax.experimental import pallas as pl
from jax.experimental.pallas import tpu as pltpu
from jax.sharding import PartitionSpec as P

HD = 128
STEPS = 3
CACHE = 128


EPSILON = 1e-05
NEGATIVE = -1e30
VMEM_LIMIT = 48 * 1024 * 1024


def partner(array, axis, bit):
    return lax.ppermute(array, axis, [(i, i ^ 1 << bit) for i in range(lax.axis_size(axis))])


def tile_of(size, most):
    tile = min(size, most)
    while size % tile:
        tile //= 2
    return tile


def rotation_tables(positions, first_pair, width, head_size):
    pair_index = (first_pair + jnp.arange(width) // 2).astype(jnp.float32)
    frequency = jnp.exp(pair_index * (-2.0 * math.log(10000.0) / head_size))
    angles = positions.astype(jnp.float32)[:, None] * frequency[None, :]
    sign = jnp.where(jnp.arange(width) % 2 == 0, -1.0, 1.0)
    return jnp.cos(angles), jnp.sin(angles) * sign


def rotate(values, cosine, sine):
    copies = values.shape[1] // cosine.shape[1]
    cosine = jnp.tile(cosine, (1, copies))
    sine = jnp.tile(sine, (1, copies))
    even = (jnp.arange(values.shape[1]) % 2 == 0)[None, :]
    other = jnp.where(even, jnp.roll(values, -1, axis=1), jnp.roll(values, 1, axis=1))
    return (values * cosine + other * sine).astype(jnp.bfloat16)


def row_scaling(x_ref):
    blocks, rows, width = x_ref.shape

    def add(index, total):
        part = x_ref[index].astype(jnp.float32)
        return total + jnp.sum(part * part, axis=-1, keepdims=True)

    total = lax.fori_loop(0, blocks, add, jnp.zeros((rows, 1), jnp.float32))
    return lax.rsqrt(total / (blocks * width) + EPSILON)


def project_kernel(weight_count, x_ref, gain_ref, *refs):
    weights = refs[:weight_count]
    outs = refs[weight_count:-1]
    scale_ref = refs[-1]
    step = pl.program_id(0)

    @pl.when(step == 0)
    def _():
        scale_ref[...] = jnp.broadcast_to(row_scaling(x_ref), scale_ref.shape)
        for out in outs:
            out[...] = jnp.zeros_like(out)

    normed = x_ref[step].astype(jnp.float32) * scale_ref[:, :1] * gain_ref[step]
    normed = normed.astype(jnp.bfloat16)
    place = 0
    for weight in weights:
        if len(weight.shape) == 2:
            outs[place][...] += jnp.dot(normed, weight[...], preferred_element_type=jnp.float32)
            place += 1
        else:
            for index in range(weight.shape[0]):
                outs[place][...] += jnp.dot(
                    normed, weight[index], preferred_element_type=jnp.float32
                )
                place += 1


def project(x, gain, weights):
    blocks, rows, tile = x.shape
    specs = []
    shapes = []
    for weight in weights:
        width = weight.shape[-1]
        lead = weight.shape[:-2]
        zeros = (0,) * len(lead)
        if weight.ndim == 4:
            specs.append(
                pl.BlockSpec((None, lead[1], tile, width), lambda k: (0, 0, k, 0))
            )
            shapes.extend([(rows, width)] * lead[1])
        elif weight.ndim == 3:
            specs.append(pl.BlockSpec((lead[0], tile, width), lambda k: (0, k, 0)))
            shapes.extend([(rows, width)] * lead[0])
        else:
            specs.append(pl.BlockSpec((tile, width), lambda k: (k, 0)))
            shapes.append((rows, width))
    return pl.pallas_call(
        functools.partial(project_kernel, len(weights)),
        grid=(blocks,),
        in_specs=[
            pl.BlockSpec((blocks, rows, tile), lambda k: (0, 0, 0)),
            pl.BlockSpec((blocks, 1, tile), lambda k: (0, 0, 0)),
        ]
        + specs,
        out_specs=[pl.BlockSpec(shape, lambda k: (0, 0)) for shape in shapes],
        out_shape=[jax.ShapeDtypeStruct(shape, jnp.float32) for shape in shapes],
        scratch_shapes=[pltpu.VMEM((rows, 128), jnp.float32)],
        compiler_params=pltpu.CompilerParams(vmem_limit_bytes=VMEM_LIMIT),
    )(x, gain.reshape(blocks, 1, tile), *weights)


def out_kernel(parts, x_ref, w_ref, o_ref):
    width = w_ref.shape[1] // parts
    for part in range(parts):
        o_ref[part] = jnp.dot(
            x_ref[...],
            w_ref[:, part * width : (part + 1) * width],
            preferred_element_type=jnp.float32,
        ).astype(o_ref.dtype)


def out_project(x, weight, blocks):
    rows, depth = x.shape
    tile = weight.shape[1] // blocks
    parts = 2 if blocks % 2 == 0 else 1
    return pl.pallas_call(
        functools.partial(out_kernel, parts),
        grid=(blocks // parts,),
        in_specs=[
            pl.BlockSpec((rows, depth), lambda n: (0, 0)),
            pl.BlockSpec((depth, tile * parts), lambda n: (0, n)),
        ],
        out_specs=pl.BlockSpec((parts, rows, tile), lambda n: (n, 0, 0)),
        out_shape=jax.ShapeDtypeStruct((blocks, rows, tile), jnp.bfloat16),
        compiler_params=pltpu.CompilerParams(vmem_limit_bytes=VMEM_LIMIT),
    )(x, weight)


def logit_kernel(x_ref, gain_ref, w_ref, o_ref, normed_ref):
    blocks, rows, width = x_ref.shape

    @pl.when((pl.program_id(0) == 0) & (pl.program_id(1) == 0))
    def _():
        scaling = row_scaling(x_ref)

        def fill(index, carry):
            normed = x_ref[index].astype(jnp.float32) * scaling * gain_ref[index]
            columns = pl.ds(pl.multiple_of(index * width, width), width)
            normed_ref[:, columns] = normed.astype(jnp.bfloat16)
            return carry

        lax.fori_loop(0, blocks, fill, 0)

    o_ref[...] = lax.dot_general(
        normed_ref[...], w_ref[...], (((1,), (1,)), ((), ())), preferred_element_type=jnp.float32
    )


def logit_project(x, gain, table, most):
    blocks, rows, block_width = x.shape
    depth = blocks * block_width
    parts, width = table.shape[:2]
    tile = tile_of(width, most)
    return pl.pallas_call(
        logit_kernel,
        grid=(parts, width // tile),
        in_specs=[
            pl.BlockSpec((blocks, rows, block_width), lambda p, n: (0, 0, 0)),
            pl.BlockSpec((blocks, 1, block_width), lambda p, n: (0, 0, 0)),
            pl.BlockSpec((None, tile, depth), lambda p, n: (p, n, 0)),
        ],
        out_specs=pl.BlockSpec((None, rows, tile), lambda p, n: (p, 0, n)),
        out_shape=jax.ShapeDtypeStruct((parts, rows, width), jnp.float32),
        scratch_shapes=[pltpu.VMEM((rows, depth), jnp.bfloat16)],
        compiler_params=pltpu.CompilerParams(vmem_limit_bytes=VMEM_LIMIT),
    )(x, gain.reshape(blocks, 1, block_width), table)


def attention_weights(cached_scores, fresh_scores, visible, causal):
    factor = 1.0 / math.sqrt(HD)
    cached_scores = jnp.where(visible, cached_scores * factor, NEGATIVE)
    fresh_scores = jnp.where(causal, fresh_scores * factor, NEGATIVE)
    row_max = jnp.maximum(
        jnp.max(cached_scores, axis=-1, keepdims=True),
        jnp.max(fresh_scores, axis=-1, keepdims=True),
    )
    cached_exp = jnp.exp(cached_scores - row_max)
    fresh_exp = jnp.exp(fresh_scores - row_max)
    totals = jnp.sum(cached_exp, axis=-1, keepdims=True) + jnp.sum(
        fresh_exp, axis=-1, keepdims=True
    )
    return ((cached_exp / totals).astype(jnp.bfloat16), (fresh_exp / totals).astype(jnp.bfloat16))


def flips(index, bits):
    return [bit * (1 - 2 * (lax.div(index, bit) % 2)) for bit in bits]


def span(offsets):
    sums = [0]
    for offset in offsets:
        sums = sums + [total + offset for total in sums]
    return sums


def link_order(size, group):
    count = size.bit_length() - 1
    first = list(reversed(range(count)))
    second = [0] + list(reversed(range(1, count))) if count else []
    return [(1 << a) + group * ((1 << b) - (1 << a)) for a, b in zip(first, second)]


def greet(partners):
    barrier = pltpu.get_barrier_semaphore()
    for target in partners:
        pl.semaphore_signal(
            barrier, inc=1, device_id=target, device_id_type=pl.DeviceIdType.MESH
        )
    pl.semaphore_wait(barrier, len(partners))


def send(source, target, sends, receives, place, device):
    copy = pltpu.make_async_remote_copy(
        src_ref=source,
        dst_ref=target,
        send_sem=sends.at[place],
        recv_sem=receives.at[place],
        device_id=device,
        device_id_type=pl.DeviceIdType.MESH,
    )
    copy.start()
    return copy


def gather_kernel(size, x_ref, o_ref, local_sem, sends, receives, core_sends, core_receives):
    group = lax.axis_index("grp")
    mine = lax.axis_index("tp")
    data = lax.axis_index("dp")
    offsets = flips(mine, link_order(size, group))
    other_core = (1 - group, mine, data)
    greet([(group, mine + offset, data) for offset in offsets] + [other_core])
    base = group * size
    keep = pltpu.make_async_copy(x_ref, o_ref.at[base + mine], local_sem)
    keep.start()
    keep.wait()
    held = [0]
    place = 0
    waiting = []
    swaps = [
        send(o_ref.at[base + mine], o_ref.at[base + mine], core_sends, core_receives, 0, other_core)
    ]
    for offset in offsets:
        copies = []
        for inner in held:
            block = base + mine + inner
            copies.append(
                send(
                    o_ref.at[block],
                    o_ref.at[block],
                    sends,
                    receives,
                    place,
                    (group, mine + offset, data),
                )
            )
            place += 1
        arrived = [inner + offset for inner in held]
        for copy, inner in zip(copies, arrived):
            copy.wait_recv()
            block = base + mine + inner
            swaps.append(
                send(
                    o_ref.at[block],
                    o_ref.at[block],
                    core_sends,
                    core_receives,
                    len(swaps),
                    other_core,
                )
            )
        waiting.extend(copies)
        held = held + arrived
    for copy in waiting:
        copy.wait_send()
    for copy in swaps:
        copy.wait()


def gather_blocks(block, identity):
    size = lax.axis_size("tp")
    count = lax.axis_size("grp") * size
    return pl.pallas_call(
        functools.partial(gather_kernel, size),
        in_specs=[pl.BlockSpec(memory_space=pltpu.VMEM)],
        out_specs=pl.BlockSpec(memory_space=pltpu.VMEM),
        out_shape=jax.ShapeDtypeStruct((count,) + block.shape, block.dtype),
        scratch_shapes=[
            pltpu.SemaphoreType.DMA(()),
            pltpu.SemaphoreType.DMA((size,)),
            pltpu.SemaphoreType.DMA((size,)),
            pltpu.SemaphoreType.DMA((size,)),
            pltpu.SemaphoreType.DMA((size,)),
        ],
        compiler_params=pltpu.CompilerParams(
            collective_id=identity, has_side_effects=True, vmem_limit_bytes=VMEM_LIMIT
        ),
    )(block)


def scatter_kernel(
    size, p_ref, x_ref, o_ref, total, stage, core_box, box, core_sends, core_receives, sends, receives
):
    group = lax.axis_index("grp")
    mine = lax.axis_index("tp")
    data = lax.axis_index("dp")
    offsets = flips(mine, list(reversed(link_order(size, group))))
    other_core = (1 - group, mine, data)
    greet([(group, mine + offset, data) for offset in offsets] + [other_core])
    order = list(reversed(span(list(reversed(offsets)))))
    swaps = [
        send(
            p_ref.at[(1 - group) * size + mine + inner_other],
            core_box.at[place],
            core_sends,
            core_receives,
            place,
            other_core,
        )
        for place, inner_other in enumerate(
            list(reversed(span(list(reversed(other_offsets(size, group, mine))))))
        )
    ]
    copies = []
    place = 0
    half = size // 2
    for index, inner in enumerate(order):
        swaps[index].wait_recv()
        value = p_ref[group * size + mine + inner].astype(jnp.float32)
        value = value + core_box[index].astype(jnp.float32)
        total[index] = value
        if size > 1 and index < half:
            stage[index] = value.astype(stage.dtype)
            copies.append(
                send(
                    stage.at[index],
                    box.at[place],
                    sends,
                    receives,
                    place,
                    (group, mine + offsets[0], data),
                )
            )
            place += 1
    first = half
    start = 0
    for phase in range(len(offsets)):
        active = size - first
        for index in range(active):
            copies[start + index].wait_recv()
            value = total[first + index] + box[start + index].astype(jnp.float32)
            total[first + index] = value
            if active > 1 and index < active // 2:
                stage[first + index] = value.astype(stage.dtype)
                copies.append(
                    send(
                        stage.at[first + index],
                        box.at[place],
                        sends,
                        receives,
                        place,
                        (group, mine + offsets[phase + 1], data),
                    )
                )
                place += 1
        start += active
        first += active // 2
    hidden = x_ref[...].astype(jnp.float32) + total[size - 1]
    o_ref[...] = hidden.astype(o_ref.dtype)
    for copy in copies + swaps:
        copy.wait_send()


def other_offsets(size, group, mine):
    return flips(mine, list(reversed(link_order(size, 1 - group))))


def scatter_blocks(partial, inputs, identity):
    size = lax.axis_size("tp")
    block = inputs.shape
    whole = pl.BlockSpec(memory_space=pltpu.VMEM)
    return pl.pallas_call(
        functools.partial(scatter_kernel, size),
        in_specs=[whole, whole],
        out_specs=whole,
        out_shape=jax.ShapeDtypeStruct(block, inputs.dtype),
        scratch_shapes=[
            pltpu.VMEM((size,) + block, jnp.float32),
            pltpu.VMEM((size,) + block, partial.dtype),
            pltpu.VMEM((size,) + block, partial.dtype),
            pltpu.VMEM((size,) + block, partial.dtype),
            pltpu.SemaphoreType.DMA((size,)),
            pltpu.SemaphoreType.DMA((size,)),
            pltpu.SemaphoreType.DMA((size,)),
            pltpu.SemaphoreType.DMA((size,)),
        ],
        compiler_params=pltpu.CompilerParams(
            collective_id=identity, has_side_effects=True, vmem_limit_bytes=VMEM_LIMIT
        ),
    )(partial, inputs)


def share_kernel(size, count, x_ref, o_ref, sends, receives):
    data = lax.axis_index("dp")
    mine = lax.axis_index("grp") * size + lax.axis_index("tp")
    others = [(mine + step) % count for step in range(1, count)]
    devices = [(other // size, other % size, data) for other in others]
    greet(devices)
    copies = [
        send(x_ref, o_ref.at[mine], sends, receives, place, device)
        for place, device in enumerate(devices)
    ]
    o_ref[mine] = x_ref[...]
    for copy in copies:
        copy.wait()


def share_small(values, identity):
    size = lax.axis_size("tp")
    count = lax.axis_size("grp") * size
    whole = pl.BlockSpec(memory_space=pltpu.VMEM)
    return pl.pallas_call(
        functools.partial(share_kernel, size, count),
        in_specs=[whole],
        out_specs=whole,
        out_shape=jax.ShapeDtypeStruct((count,) + values.shape, values.dtype),
        scratch_shapes=[
            pltpu.SemaphoreType.DMA((count - 1,)),
            pltpu.SemaphoreType.DMA((count - 1,)),
        ],
        compiler_params=pltpu.CompilerParams(collective_id=identity, has_side_effects=True),
    )(values)


def body(
    base_inputs,
    small_inputs,
    base_norm_gain,
    base_query,
    base_keys_values,
    base_output,
    base_cache,
    base_final_gain,
    base_unembed,
    small_norm_gain,
    small_projections,
    small_output,
    small_cache,
    small_final_gain,
    small_unembed,
    lengths,
    next_tokens,
):
    row_count = lengths.shape[0]
    total_rows = STEPS * row_count
    slice_width = base_keys_values.shape[2]
    share_count = HD // slice_width
    group_size = base_query.shape[1] // slice_width
    slice_index = lax.axis_index("tp") % share_count
    first_pair = slice_index * (slice_width // 2)
    block_index = lax.axis_index("grp") * lax.axis_size("tp") + lax.axis_index("tp")
    vocab_width = base_unembed.shape[0]
    small_heads = small_projections.shape[3] // HD
    small_block = small_inputs.reshape(total_rows, -1)
    base_block = base_inputs.reshape(total_rows, -1)
    small_full = lax.all_gather(small_block, "tp", axis=0)
    base_full = gather_blocks(base_block, 0)
    positions = (jnp.arange(STEPS)[:, None] + lengths[None, :]).reshape(-1)
    visible = (jnp.arange(CACHE)[None, :] < lengths[:, None])[:, None, None, :]
    step_range = jnp.arange(STEPS)
    causal = step_range[None, :] <= step_range[:, None]

    small_q, small_k, small_v = project(
        small_full, small_norm_gain, [small_projections]
    )
    cosine, sine = rotation_tables(positions, 0, HD, HD)
    by_head = (STEPS, row_count, small_heads, HD)
    small_q = rotate(small_q, cosine, sine).reshape(by_head)
    small_k = rotate(small_k, cosine, sine).reshape(by_head)
    small_v = small_v.astype(jnp.bfloat16).reshape(by_head)
    keys = small_cache[0, 0].reshape(row_count, small_heads, HD, CACHE)
    values = small_cache[0, 1].reshape(row_count, small_heads, HD, CACHE)
    cached = jnp.einsum("srhd,rhdl->rhsl", small_q, keys, preferred_element_type=jnp.float32)
    fresh = jnp.einsum("srhd,nrhd->rhsn", small_q, small_k, preferred_element_type=jnp.float32)
    cached, fresh = attention_weights(cached, fresh, visible, causal[None, None])
    heads = jnp.einsum("rhsl,rhdl->srhd", cached, values, preferred_element_type=jnp.float32)
    heads = heads + jnp.einsum(
        "rhsn,nrhd->srhd", fresh, small_v, preferred_element_type=jnp.float32
    )
    heads = heads.astype(jnp.bfloat16).reshape(total_rows, small_heads * HD)
    small_partial = out_project(heads, small_output[0], small_full.shape[0])
    small_mixed = lax.psum_scatter(small_partial, "tp", scatter_dimension=0, tiled=False)
    small_hidden = small_block.astype(jnp.float32) + small_mixed.astype(jnp.float32)
    small_hidden = lax.all_gather(small_hidden.astype(jnp.bfloat16), "tp", axis=0)
    small_logits = logit_project(small_hidden, small_final_gain, small_unembed[0], 512)
    group = lax.axis_index("grp")
    own = lax.dynamic_index_in_dim(small_logits, group, 0, keepdims=False)
    theirs = lax.dynamic_index_in_dim(small_logits, 1 - group, 0, keepdims=False)
    received = lax.ppermute(theirs, "grp", [(0, 1), (1, 0)])

    query, new_key, new_value = project(
        base_full, base_norm_gain, [base_query, base_keys_values]
    )
    cosine, sine = rotation_tables(positions, first_pair, slice_width, HD)
    query = rotate(query, cosine, sine).reshape(STEPS, row_count, group_size, slice_width)
    new_key = rotate(new_key, cosine, sine).reshape(STEPS, row_count, slice_width)
    new_value = new_value.astype(jnp.bfloat16).reshape(STEPS, row_count, slice_width)
    cached = jnp.einsum("srgd,rdl->rsgl", query, base_cache[0], preferred_element_type=jnp.float32)
    fresh = jnp.einsum("srgd,nrd->rsgn", query, new_key, preferred_element_type=jnp.float32)
    for bit in range(share_count.bit_length() - 1):
        cached = cached + partner(cached, "tp", bit)
        fresh_flat = fresh.reshape(row_count, -1)
        fresh = fresh + partner(fresh_flat, "tp", bit).reshape(fresh.shape)
    cached, fresh = attention_weights(cached, fresh, visible, causal[:, None, :][None])
    heads = jnp.einsum("rsgl,rdl->srgd", cached, base_cache[1], preferred_element_type=jnp.float32)
    heads = heads + jnp.einsum(
        "rsgn,nrd->srgd", fresh, new_value, preferred_element_type=jnp.float32
    )
    heads = heads.astype(jnp.bfloat16).reshape(total_rows, group_size * slice_width)
    partial = out_project(heads, base_output, base_full.shape[0])
    hidden = gather_blocks(scatter_blocks(partial, base_block, 1), 2)
    base_logits = logit_project(hidden, base_final_gain, base_unembed[None], 256)[0]
    gap = jnp.where(group == 0, own - received, received - own)
    steered = base_logits + gap

    local_max = jnp.max(steered, axis=-1)
    local_total = jnp.sum(jnp.exp(steered - local_max[:, None]), axis=-1)
    token_local = next_tokens.reshape(-1) - block_index * vocab_width
    token_hit = jnp.arange(vocab_width)[None, :] == token_local[:, None]
    picked = jnp.sum(jnp.where(token_hit, steered, 0.0), axis=-1)
    packed = jnp.stack([local_max, local_total, picked])
    packed = jnp.pad(packed, ((0, -3 % 8), (0, -total_rows % 128)))
    stats = share_small(packed, 3)[:, :3, :total_rows]
    row_max = jnp.max(stats[:, 0], axis=0)
    exp_total = jnp.sum(stats[:, 1] * jnp.exp(stats[:, 0] - row_max[None]), axis=0)
    log_norm = row_max + jnp.log(exp_total)
    chosen = jnp.sum(stats[:, 2], axis=0) - log_norm
    log_probs = steered - log_norm[:, None]
    return (
        log_probs.reshape(STEPS, row_count, vocab_width),
        jnp.sum(chosen.reshape(STEPS, row_count), axis=0),
    )


def solution(mesh):
    placed = (
        P(None, "dp", ("grp", "tp")),
        P("grp", None, "dp", "tp"),
        P(),
        P(None, ("grp", "tp")),
        P(None, None, ("grp", "tp")),
        P(("grp", "tp"), None),
        P(None, "dp", ("grp", "tp"), None),
        P(),
        P(("grp", "tp"), None),
        P("grp", None),
        P("grp", None, None, "tp"),
        P("grp", "tp", None),
        P("grp", None, "dp", "tp", None),
        P("grp", None),
        P("grp", None, "tp", None),
        P("dp"),
        P(None, "dp"),
    )
    return jax.shard_map(
        body,
        mesh=mesh,
        in_specs=placed,
        out_specs=(P(None, "dp", ("grp", "tp")), P("dp")),
        check_vma=False,
    )
```
